512 devices in a mesh: dp: 16 (over x_hi, y, core), mp: 32 (over z, x_lo).
Axes of the slice: x: 4 (x_hi: 2, x_lo: 2; x = x_hi * 2 + x_lo), y: 4, z: 16, core: 2. Of those that a mesh axis runs over, the one named last changes fastest.
Arguments:
- inputs: bfloat16 [8192, 32768], P('dp', 'mp'), may hold values from -6 to 6
- cotangent: bfloat16 [8192, 32768], P('dp', 'mp'), may hold values from -6 to 6
- first_diag: bfloat16 [64, 512, 512], P('mp', 'dp'), may hold values from -0.1875 to 0.1875
- first_cross: bfloat16 [64, 512, 512], P('mp', 'dp'), may hold values from -0.1875 to 0.1875
- second_diag: bfloat16 [64, 512, 512], P('mp', 'dp'), may hold values from -0.1875 to 0.1875
- second_cross: bfloat16 [64, 512, 512], P('mp', 'dp'), may hold values from -0.1875 to 0.1875
Outputs:
- output: bfloat16 [8192, 32768], P('dp', 'mp')
- input_grad: bfloat16 [8192, 32768], P('dp', 'mp')
- grad_first_diag: float32 [64, 512, 512], P('mp', 'dp')
- grad_first_cross: float32 [64, 512, 512], P('mp', 'dp')
- grad_second_diag: float32 [64, 512, 512], P('mp', 'dp')
- grad_second_cross: float32 [64, 512, 512], P('mp', 'dp')
The draws below stay inside these ranges and needn't reach their ends.
All inputs are finite; a program needn't handle non-finite values.
Results may differ from the reference program's by a relative error of at most 0.02.
Values may be sent and summed in bfloat16 or wider, within the bound.
A program may use at most 64 MiB of HBM per device.

```python
import math
import jax
import jax.numpy as jnp
import numpy as np
from jax import lax

B = 512
TOK_DEV = 512
NBLK = 64
HID = 32768
TOKENS = 8192
N_DP = 16
N_MP = 32


def with_spikes(drawn, rng, source, target, shards_of, factor):
    def block_of(dim):
        return (jnp.arange(drawn.shape[dim]) // (drawn.shape[dim] // shards_of)).reshape((-1,) + (1,) * (drawn.ndim - 1 - dim))

    near = jax.random.permutation(rng, shards_of)[block_of(target)]
    far = (block_of(target) + shards_of // 2) % shards_of
    return jnp.where((block_of(source) == near) | (block_of(source) == far), factor * drawn, drawn)


def block_scale(key, dims, cuts, least, top_value):
    loudness = 1.0
    for dim, blocks in cuts:
        steps = jax.random.uniform(jax.random.fold_in(jax.random.fold_in(key, 6), dim), (blocks,), jnp.float32, least / len(cuts), top_value / len(cuts))
        loudness = loudness * jnp.repeat(jnp.exp(steps), dims[dim] // blocks).reshape((-1,) + (1,) * (len(dims) - 1 - dim))
    return loudness


def gaussian(own_key, shape, spread, limit, split=(), dtype=jnp.bfloat16):
    entries = jax.random.normal(own_key, shape, jnp.float32) * spread
    if len(split) > 0:
        entries = block_scale(own_key, shape, split, -0.22, 0.18) * entries
    return jnp.clip(entries, min=-limit, max=limit).astype(dtype)


def heavy_noise(own_key, shape, scale, bound, shards, heavy, kind=jnp.bfloat16):
    values = scale * jax.random.normal(own_key, shape, jnp.float32)
    if shards:
        values = values * block_scale(own_key, shape, shards, -0.22, 0.18)
    return jnp.clip(with_spikes(values, jax.random.fold_in(own_key, 3), *heavy), -bound, bound).astype(kind)


def setup_inputs(seed: int = 0) -> dict:
    keys = jax.random.split(jax.random.key(seed), 7)
    return {
        "inputs": heavy_noise(keys[0], (TOKENS, HID), 1.0, 6.0, ((0, 16), (1, 32)), (0, 1, 32, 2.75)),
        "cotangent": gaussian(keys[1], (TOKENS, HID), 1.0, 6.0, ((0, 16), (1, 32))),
        "first_diag": gaussian(keys[2], (NBLK, B, B), (2 * B) ** -0.5, 0.1875, ((0, 32), (1, 16))),
        "first_cross": gaussian(keys[3], (NBLK, B, B), (2 * B) ** -0.5, 0.1875, ((0, 32), (1, 16))),
        "second_diag": gaussian(keys[4], (NBLK, B, B), (2 * B) ** -0.5, 0.1875, ((0, 32), (1, 16))),
        "second_cross": gaussian(keys[5], (NBLK, B, B), (2 * B) ** -0.5, 0.1875, ((0, 32), (1, 16))),
    }


def gelu_value(value):
    return value * 0.5 * (1.0 + jax.scipy.special.erf(value / math.sqrt(2.0)))

def gelu_slope(value):
    cumul = 0.5 * (1.0 + jax.scipy.special.erf(value / math.sqrt(2.0)))
    return cumul + value * jnp.exp(-0.5 * value * value) / math.sqrt(2.0 * math.pi)

def apply_blocks(left, weight):
    return jnp.einsum('tkb,kbc->tkc', left.astype(jnp.float32), weight.astype(jnp.float32))

def apply_blocks_t(left, weight):
    return jnp.einsum('tkc,kbc->tkb', left.astype(jnp.float32), weight.astype(jnp.float32))

def group_sum(left, right):
    block_count = 2 * N_MP
    lhs = jnp.moveaxis(left.reshape(N_DP, TOK_DEV, block_count, B), 2, 0)
    rhs = jnp.moveaxis(right.reshape(N_DP, TOK_DEV, block_count, B), 2, 0)

    def one_block(pair):
        lpart, rpart = pair
        parts = jnp.einsum('gtb,gtc->gbc', lpart.astype(jnp.float32), rpart.astype(jnp.float32))
        rounded = lax.optimization_barrier(parts.astype(jnp.bfloat16))
        return lax.optimization_barrier(jnp.sum(rounded.astype(jnp.float32), axis=0))
    return lax.map(one_block, (lhs, rhs))

def reference(inputs, cotangent, first_diag, first_cross, second_diag, second_cross):
    block_count = 2 * N_MP
    other_first = np.arange(block_count) ^ 2
    other_second = np.arange(block_count) ^ N_MP
    inputs_blk = inputs.reshape(TOKENS, block_count, B)
    cot_blk = cotangent.reshape(TOKENS, block_count, B)
    inputs_other = inputs_blk[:, other_first, :]
    hidden_pre = apply_blocks(inputs_blk, first_diag) + apply_blocks(inputs_other, first_cross)
    hidden_act = gelu_value(hidden_pre).astype(jnp.bfloat16)
    hidden_other = hidden_act[:, other_second, :]
    output = (apply_blocks(hidden_act, second_diag) + apply_blocks(hidden_other, second_cross)).astype(jnp.bfloat16)
    back_second = apply_blocks_t(cot_blk, second_cross).astype(jnp.bfloat16)
    hidden_grad = apply_blocks_t(cot_blk, second_diag) + back_second[:, other_second, :].astype(jnp.float32)
    pre_grad = (hidden_grad * gelu_slope(hidden_pre)).astype(jnp.bfloat16)
    back_first = apply_blocks_t(pre_grad, first_cross).astype(jnp.bfloat16)
    input_grad = (apply_blocks_t(pre_grad, first_diag) + back_first[:, other_first, :].astype(jnp.float32)).astype(jnp.bfloat16)
    grad_second_diag = group_sum(hidden_act, cot_blk)
    grad_second_cross = group_sum(hidden_other, cot_blk)
    grad_first_diag = group_sum(inputs_blk, pre_grad)
    grad_first_cross = group_sum(inputs_other, pre_grad)
    return (output.reshape(TOKENS, block_count * B), input_grad.reshape(TOKENS, block_count * B), grad_first_diag, grad_first_cross, grad_second_diag, grad_second_cross)
```

```python
import math

import jax
import jax.numpy as jnp
from jax import lax
from jax.experimental import pallas as pl
from jax.experimental.pallas import tpu as pltpu
from jax.sharding import PartitionSpec as P

MESH = pl.DeviceIdType.MESH
BF16 = jnp.bfloat16
F32 = jnp.float32
FD, FC, SD, SC = range(4)


def mm(left, right):
    return lax.dot_general(left, right, (((1,), (0,)), ((), ())), preferred_element_type=F32)


def mm_nt(left, right):
    return lax.dot_general(left, right, (((1,), (1,)), ((), ())), preferred_element_type=F32)


def mm_tn(left, right):
    return lax.dot_general(left, right, (((0,), (0,)), ((), ())), preferred_element_type=F32)


def make_kernel(n_dp, n_mp, rows, width, shard):
    tile = min(128, rows)
    n_tiles = rows // tile
    col_tile = min(256, width)
    n_cols = width // col_tile

    def kernel(
        x_hbm, c_hbm, fd_hbm, fc_hbm, sd_hbm, sc_hbm,
        out_hbm, ig_hbm, gfd_hbm, gfc_hbm, gsd_hbm, gsc_hbm,
        x_v, c_v, w_v, scq_v, xo_v, cq_v, bs_out, bs_in, slope_v, h_v, ho_v, pg_v, bf_out, bf_in,
        out_v, ig_v, part_v, rs_v, grad_v, gq_out, gq_in,
        loc_sem, ag_send, ag_recv, fw_send, fw_recv, z_send, z_recv, xs_send, xs_recv,
        rs_send, rs_recv, st_sem,
    ):
        dp = lax.axis_index("dp")
        mp = lax.axis_index("mp")
        zp = lax.rem(mp + n_mp // 2, n_mp)
        xp = mp + 1 - 2 * lax.rem(mp, 2)
        to_z = {"mp": zp}
        to_x = {"mp": xp}

        def peer(step):
            return lax.rem(dp + step, n_dp)

        def cols(k):
            return pl.ds(k * width, width)

        def shard_rows(index):
            return pl.ds(pl.multiple_of(index * shard, shard), shard)

        def remote(src, dst, ssem, rsem, device):
            return pltpu.make_async_remote_copy(
                src_ref=src, dst_ref=dst, send_sem=ssem, recv_sem=rsem, device_id=device, device_id_type=MESH
            )

        def each_peer(body):
            def step(d, carry):
                body(d)
                return carry

            lax.fori_loop(1, n_dp, step, 0)

        def each_tile(body):
            def step(t, carry):
                body(pl.ds(pl.multiple_of(t * tile, tile), tile))
                return carry

            lax.fori_loop(0, n_tiles, step, 0)

        shards = (fd_hbm, fc_hbm, sd_hbm, sc_hbm)
        load_w = [
            pltpu.make_async_copy(shards[f], w_v.at[f, :, shard_rows(dp), :], loc_sem.at[f]) for f in range(4)
        ]
        load_c = pltpu.make_async_copy(c_hbm, c_v, loc_sem.at[4])
        load_x = pltpu.make_async_copy(x_hbm, x_v, loc_sem.at[5])
        for load in (load_w[SC], load_c, load_x, load_w[FD], load_w[FC], load_w[SD]):
            load.start()

        barrier = pltpu.get_barrier_semaphore()
        pl.semaphore_signal(barrier, inc=1, device_id=to_z, device_id_type=MESH)
        pl.semaphore_signal(barrier, inc=1, device_id=to_x, device_id_type=MESH)
        each_peer(lambda d: pl.semaphore_signal(barrier, inc=1, device_id={"dp": peer(d)}, device_id_type=MESH))
        pl.semaphore_wait(barrier, n_dp + 1)

        def gather(f, owner, target):
            view = w_v.at[f, :, shard_rows(owner), :]
            return remote(view, view, ag_send.at[f, target], ag_recv.at[f, owner], {"dp": target})

        def gather_q(owner, target):
            view = scq_v.at[shard_rows(owner), :]
            return remote(view, view, fw_send.at[target], fw_recv.at[owner], {"dp": target})

        def gather_start(f):
            each_peer(lambda d: gather(f, dp, peer(d)).start())

        def gather_wait(f):
            each_peer(lambda d: gather(f, peer(d), peer(d)).wait_recv())

        z_shard = remote(
            w_v.at[SC, 0, shard_rows(dp), :], scq_v.at[shard_rows(dp), :], z_send.at[0], z_recv.at[0], to_z
        )
        z_cot = remote(c_v.at[:, cols(0)], cq_v, z_send.at[1], z_recv.at[1], to_z)
        z_back = remote(bs_out, bs_in, z_send.at[2], z_recv.at[2], to_z)
        z_hid = [
            remote(h_v.at[:, cols(k)], ho_v.at[:, cols(k)], z_send.at[3 + k], z_recv.at[3 + k], to_z) for k in (0, 1)
        ]
        z_grad = remote(gq_out, gq_in, z_send.at[5], z_recv.at[5], to_z)
        x_in = remote(x_v, xo_v, xs_send.at[0], xs_recv.at[0], to_x)
        x_back = [
            remote(bf_out.at[:, cols(k)], bf_in.at[:, cols(k)], xs_send.at[1 + k], xs_recv.at[1 + k], to_x)
            for k in (0, 1)
        ]

        load_w[SC].wait()
        z_shard.start()
        load_c.wait()
        z_cot.start()
        gather_start(SC)
        load_x.wait()
        x_in.start()
        load_w[FD].wait()
        gather_start(FD)
        load_w[FC].wait()
        gather_start(FC)
        z_shard.wait_recv()
        each_peer(lambda d: gather_q(dp, peer(d)).start())
        load_w[SD].wait()
        gather_start(SD)

        gather_wait(SC)

        def back_second(r):
            bs_out[r, :] = mm_nt(c_v[r, cols(1)], w_v[SC, 1]).astype(BF16)

        each_tile(back_second)
        z_back.start()

        def scatter(f, k, source, target):
            return remote(
                part_v.at[f, k, shard_rows(target), :], rs_v.at[f, k, source],
                rs_send.at[f, k, target], rs_recv.at[f, k, source], {"dp": target},
            )

        def outer(f, k, left, right):
            def step(j, carry):
                b = pl.ds(pl.multiple_of(j * col_tile, col_tile), col_tile)
                lb = pl.ds(pl.multiple_of(k * width + j * col_tile, col_tile), col_tile)
                part_v[f, k, b, :] = mm_tn(left[:, lb], right()).astype(BF16)
                return carry

            lax.fori_loop(0, n_cols, step, 0)
            each_peer(lambda d: scatter(f, k, dp, peer(d)).start())

        def reduced(f, k):
            each_peer(lambda d: scatter(f, k, peer(d), peer(d)).wait_recv())
            own = part_v[f, k, shard_rows(dp), :].astype(F32)

            def add(d, total):
                return total + rs_v[f, k, peer(d)].astype(F32)

            return lax.fori_loop(1, n_dp, add, own)

        gather_wait(FD)
        gather_wait(FC)
        x_in.wait_recv()

        for k in (0, 1):
            def hidden(r, k=k):
                pre = mm(x_v[r, cols(k)], w_v[FD, k]) + mm(xo_v[r, cols(k)], w_v[FC, k])
                cumul = 0.5 * (1.0 + lax.erf(pre * (1.0 / math.sqrt(2.0))))
                h_v[r, cols(k)] = (pre * cumul).astype(BF16)
                slope_v[r, cols(k)] = cumul + pre * jnp.exp(-0.5 * pre * pre) * (1.0 / math.sqrt(2.0 * math.pi))

            each_tile(hidden)

        for k in (0, 1):
            outer(SD, k, h_v, lambda k=k: c_v[:, cols(k)])

        z_cot.wait_recv()
        z_hid[1].start()
        outer(SC, 0, h_v, lambda: cq_v[...])

        gather_wait(SD)
        each_peer(lambda d: gather_q(peer(d), peer(d)).wait_recv())

        def first_section(k):
            def grads(r):
                if k == 0:
                    from_partner = mm_nt(cq_v[r, :], scq_v[...])
                else:
                    from_partner = bs_in[r, :].astype(F32)
                total = mm_nt(c_v[r, cols(k)], w_v[SD, k]) + from_partner
                pre_grad = (total * slope_v[r, cols(k)]).astype(BF16)
                pg_v[r, cols(k)] = pre_grad
                bf_out[r, cols(k)] = mm_nt(pre_grad, w_v[FC, k]).astype(BF16)

            each_tile(grads)
            x_back[k].start()
            outer(FD, k, x_v, lambda: pg_v[:, cols(k)])
            outer(FC, k, xo_v, lambda: pg_v[:, cols(k)])

        first_section(0)
        z_back.wait_recv()
        z_hid[0].start()
        first_section(1)

        gq_out[...] = reduced(SC, 0).astype(BF16)
        z_grad.start()

        stores = []

        def store(src, dst):
            copy = pltpu.make_async_copy(src, dst, st_sem.at[len(stores)])
            copy.start()
            stores.append(copy)

        for k in (0, 1):
            x_back[k].wait_recv()

            def input_grad(r, k=k):
                total = mm_nt(pg_v[r, cols(k)], w_v[FD, k]) + bf_in[r, cols(k)].astype(F32)
                ig_v[r, cols(k)] = total.astype(BF16)

            each_tile(input_grad)
        store(ig_v, ig_hbm)

        def output(k):
            def rows_of(r):
                total = mm(h_v[r, cols(k)], w_v[SD, k]) + mm(ho_v[r, cols(k)], w_v[SC, k])
                out_v[r, cols(k)] = total.astype(BF16)

            each_tile(rows_of)
            store(out_v.at[:, cols(k)], out_hbm.at[:, cols(k)])

        for f, g_hbm in ((SD, gsd_hbm), (FD, gfd_hbm), (FC, gfc_hbm)):
            for k in (0, 1):
                grad_v[f, k] = reduced(f, k)
            store(grad_v.at[f], g_hbm)

        z_hid[1].wait_recv()
        outer(SC, 1, ho_v, lambda: c_v[:, cols(1)])
        output(1)
        grad_v[SC, 1] = reduced(SC, 1)
        z_grad.wait_recv()
        grad_v[SC, 0] = gq_in[...].astype(F32)
        store(grad_v.at[SC], gsc_hbm)
        z_hid[0].wait_recv()
        output(0)

        for f in range(4):
            each_peer(lambda d, f=f: gather(f, dp, peer(d)).wait_send())
            for k in (0, 1):
                each_peer(lambda d, f=f, k=k: scatter(f, k, dp, peer(d)).wait_send())
        each_peer(lambda d: gather_q(dp, peer(d)).wait_send())
        for copy in (z_shard, z_cot, z_back, *z_hid, z_grad, x_in, *x_back):
            copy.wait_send()
        for copy in stores:
            copy.wait()

    wide = (rows, 2 * width)
    dma = pltpu.SemaphoreType.DMA
    scratch = [
        pltpu.VMEM(wide, BF16),
        pltpu.VMEM(wide, BF16),
        pltpu.VMEM((4, 2, width, width), BF16),
        pltpu.VMEM((width, width), BF16),
        pltpu.VMEM(wide, BF16),
        pltpu.VMEM((rows, width), BF16),
        pltpu.VMEM((rows, width), BF16),
        pltpu.VMEM((rows, width), BF16),
        pltpu.VMEM(wide, F32),
        pltpu.VMEM(wide, BF16),
        pltpu.VMEM(wide, BF16),
        pltpu.VMEM(wide, BF16),
        pltpu.VMEM(wide, BF16),
        pltpu.VMEM(wide, BF16),
        pltpu.VMEM(wide, BF16),
        pltpu.VMEM(wide, BF16),
        pltpu.VMEM((4, 2, width, width), BF16),
        pltpu.VMEM((4, 2, n_dp, shard, width), BF16),
        pltpu.VMEM((4, 2, shard, width), F32),
        pltpu.VMEM((shard, width), BF16),
        pltpu.VMEM((shard, width), BF16),
        dma((6,)),
        dma((4, n_dp)),
        dma((4, n_dp)),
        dma((n_dp,)),
        dma((n_dp,)),
        dma((6,)),
        dma((6,)),
        dma((3,)),
        dma((3,)),
        dma((4, 2, n_dp)),
        dma((4, 2, n_dp)),
        dma((7,)),
    ]
    return kernel, scratch


def solution(mesh):
    n_dp, n_mp = mesh.shape["dp"], mesh.shape["mp"]

    def local(*args):
        rows, two_width = args[0].shape
        shard, width = args[2].shape[1:]
        kernel, scratch = make_kernel(n_dp, n_mp, rows, width, shard)
        act = jax.ShapeDtypeStruct((rows, two_width), BF16)
        grad = jax.ShapeDtypeStruct((2, shard, width), F32)
        hbm = pl.BlockSpec(memory_space=pl.ANY)
        return pl.pallas_call(
            kernel,
            out_shape=(act, act, grad, grad, grad, grad),
            in_specs=[hbm] * 6,
            out_specs=[hbm] * 6,
            scratch_shapes=scratch,
            compiler_params=pltpu.CompilerParams(
                collective_id=0, has_side_effects=True, vmem_limit_bytes=48 * 1024 * 1024
            ),
            name="butterfly",
        )(*args)

    tokens = P("dp", "mp")
    blocks = P("mp", "dp", None)
    specs = (tokens, tokens, blocks, blocks, blocks, blocks)
    return jax.shard_map(local, mesh=mesh, in_specs=specs, out_specs=specs, check_vma=False)
```

```python
import math

import jax
import jax.numpy as jnp
from jax import lax
from jax.experimental import pallas as pl
from jax.experimental.pallas import tpu as pltpu
from jax.sharding import PartitionSpec as P

MESH = pl.DeviceIdType.MESH
BF16 = jnp.bfloat16
F32 = jnp.float32
FD, FC, SD, SC = range(4)


def mm(left, right):
    return lax.dot_general(left, right, (((1,), (0,)), ((), ())), preferred_element_type=F32)


def mm_nt(left, right):
    return lax.dot_general(left, right, (((1,), (1,)), ((), ())), preferred_element_type=F32)


def mm_tn(left, right):
    return lax.dot_general(left, right, (((0,), (0,)), ((), ())), preferred_element_type=F32)


def make_kernel(n_dp, n_mp, rows, width, shard):
    tile = min(128, rows)
    n_tiles = rows // tile
    n_chips = n_dp // 2
    col_tile = min(256, width)
    n_cols = width // col_tile

    def kernel(
        x_hbm, c_hbm, fd_hbm, fc_hbm, sd_hbm, sc_hbm,
        out_hbm, ig_hbm, gfd_hbm, gfc_hbm, gsd_hbm, gsc_hbm,
        x_v, c_v, w_v, scq_v, xo_v, cq_v, bs_out, bs_in, slope_v, h_v, ho_v, pg_v, bf_out, bf_in,
        part_v, rs_v, pair_v, out_v, ig_v, grad_v, acc_v, gq_out, gq_in,
        loc_sem, ag_send, ag_recv, fw_send, fw_recv, z_send, z_recv, xs_send, xs_recv,
        rs_send, rs_recv, tw_send, tq_send, pr_send, pr_recv, st_sem,
    ):
        dp = lax.axis_index("dp")
        mp = lax.axis_index("mp")
        zp = lax.rem(mp + n_mp // 2, n_mp)
        xp = mp + 1 - 2 * lax.rem(mp, 2)
        to_z = {"mp": zp}
        to_x = {"mp": xp}

        chip = dp // 2
        core = lax.rem(dp, 2)
        twin = dp + 1 - 2 * core
        to_twin = {"dp": twin}

        def peer(step):
            return 2 * lax.rem(chip + step, n_chips) + core

        def peer_twin(step):
            return 2 * lax.rem(chip + step, n_chips) + 1 - core

        def cols(k):
            return pl.ds(k * width, width)

        def shard_rows(index):
            return pl.ds(pl.multiple_of(index * shard, shard), shard)

        def remote(src, dst, ssem, rsem, device):
            return pltpu.make_async_remote_copy(
                src_ref=src, dst_ref=dst, send_sem=ssem, recv_sem=rsem, device_id=device, device_id_type=MESH
            )

        def each_peer(body, first=1):
            def step(d, carry):
                body(d)
                return carry

            lax.fori_loop(first, n_chips, step, 0)

        def each_tile(body):
            def step(t, carry):
                body(pl.ds(pl.multiple_of(t * tile, tile), tile))
                return carry

            lax.fori_loop(0, n_tiles, step, 0)

        shards = (fd_hbm, fc_hbm, sd_hbm, sc_hbm)
        load_w = [
            pltpu.make_async_copy(shards[f], w_v.at[f, :, shard_rows(dp), :], loc_sem.at[f]) for f in range(4)
        ]
        load_c = pltpu.make_async_copy(c_hbm, c_v, loc_sem.at[4])
        load_x = pltpu.make_async_copy(x_hbm, x_v, loc_sem.at[5])
        for load in (load_w[SC], load_c, load_x, load_w[FD], load_w[FC], load_w[SD]):
            load.start()

        barrier = pltpu.get_barrier_semaphore()
        pl.semaphore_signal(barrier, inc=1, device_id=to_z, device_id_type=MESH)
        pl.semaphore_signal(barrier, inc=1, device_id=to_x, device_id_type=MESH)
        pl.semaphore_signal(barrier, inc=1, device_id=to_twin, device_id_type=MESH)
        each_peer(lambda d: pl.semaphore_signal(barrier, inc=1, device_id={"dp": peer(d)}, device_id_type=MESH))
        pl.semaphore_wait(barrier, n_chips + 2)

        def gather(f, owner, target):
            view = w_v.at[f, :, shard_rows(owner), :]
            return remote(view, view, ag_send.at[f, target], ag_recv.at[f, owner], {"dp": target})

        def gather_q(owner, target):
            view = scq_v.at[shard_rows(owner), :]
            return remote(view, view, fw_send.at[target], fw_recv.at[owner], {"dp": target})

        def pass_on(f, owner):
            view = w_v.at[f, :, shard_rows(owner), :]
            return remote(view, view, tw_send.at[f, owner], ag_recv.at[f, owner], to_twin)

        def pass_on_q(owner):
            view = scq_v.at[shard_rows(owner), :]
            return remote(view, view, tq_send.at[owner], fw_recv.at[owner], to_twin)

        def gather_start(f):
            pass_on(f, dp).start()
            each_peer(lambda d: gather(f, dp, peer(d)).start())

        def gather_q_start():
            pass_on_q(dp).start()
            each_peer(lambda d: gather_q(dp, peer(d)).start())

        def gather_pass(f):
            def one(d):
                gather(f, peer(d), peer(d)).wait_recv()
                pass_on(f, peer(d)).start()

            each_peer(one)

        def gather_q_pass():
            def one(d):
                gather_q(peer(d), peer(d)).wait_recv()
                pass_on_q(peer(d)).start()

            each_peer(one)

        def gather_wait(f):
            each_peer(lambda d: pass_on(f, peer_twin(d)).wait_recv(), first=0)

        def gather_q_wait():
            each_peer(lambda d: pass_on_q(peer_twin(d)).wait_recv(), first=0)

        z_shard = remote(
            w_v.at[SC, 0, shard_rows(dp), :], scq_v.at[shard_rows(dp), :], z_send.at[0], z_recv.at[0], to_z
        )
        z_cot = remote(c_v.at[:, cols(0)], cq_v, z_send.at[1], z_recv.at[1], to_z)
        z_back = remote(bs_out, bs_in, z_send.at[2], z_recv.at[2], to_z)
        halves = [pl.ds(i * (rows // 2), rows // 2) for i in (0, 1)]
        z_hid = [
            [
                remote(h_v.at[r, cols(k)], ho_v.at[r, cols(k)], z_send.at[6 + 2 * k + i], z_recv.at[6 + 2 * k + i], to_z)
                for i, r in enumerate(halves)
            ]
            for k in (0, 1)
        ]
        z_grad = remote(gq_out, gq_in, z_send.at[5], z_recv.at[5], to_z)
        x_in = remote(x_v, xo_v, xs_send.at[0], xs_recv.at[0], to_x)
        x_back = [
            remote(bf_out.at[:, cols(k)], bf_in.at[:, cols(k)], xs_send.at[1 + k], xs_recv.at[1 + k], to_x)
            for k in (0, 1)
        ]

        load_w[SC].wait()
        z_shard.start()
        load_c.wait()
        z_cot.start()
        gather_start(SC)
        load_x.wait()
        x_in.start()
        load_w[FD].wait()
        gather_start(FD)
        load_w[FC].wait()
        gather_start(FC)
        z_shard.wait_recv()
        gather_q_start()
        load_w[SD].wait()
        gather_start(SD)

        gather_pass(SC)
        gather_wait(SC)

        def back_second(r):
            bs_out[r, :] = mm_nt(c_v[r, cols(1)], w_v[SC, 1]).astype(BF16)

        each_tile(back_second)
        z_back.start()

        def pair(f, k, target):
            return remote(
                part_v.at[f, k, shard_rows(target), :], pair_v.at[f, k, target // 2],
                pr_send.at[f, k, target // 2], pr_recv.at[f, k, target // 2], to_twin,
            )

        def scatter(f, k, source, target):
            return remote(
                part_v.at[f, k, shard_rows(target), :], rs_v.at[f, k, source // 2],
                rs_send.at[f, k, target // 2], rs_recv.at[f, k, source // 2], {"dp": target},
            )

        def fold_one(f, k, d):
            target = peer(d)
            pair(f, k, target).wait_recv()
            both = part_v[f, k, shard_rows(target), :].astype(F32) + pair_v[f, k, target // 2].astype(F32)
            part_v[f, k, shard_rows(target), :] = both.astype(BF16)

        def fold(f, k):
            def one(d):
                fold_one(f, k, d)
                scatter(f, k, dp, peer(d)).start()

            each_peer(one)
            fold_one(f, k, 0)

        def outer(f, k, left, right):
            def step(j, carry):
                b = pl.ds(pl.multiple_of(j * col_tile, col_tile), col_tile)
                lb = pl.ds(pl.multiple_of(k * width + j * col_tile, col_tile), col_tile)
                part_v[f, k, b, :] = mm_tn(left[:, lb], right()).astype(BF16)
                return carry

            lax.fori_loop(0, n_cols, step, 0)
            each_peer(lambda d: pair(f, k, peer_twin(d)).start(), first=0)

        def reduced(f, k):
            each_peer(lambda d: scatter(f, k, peer(d), peer(d)).wait_recv())
            own = part_v[f, k, shard_rows(dp), :].astype(F32)

            def add(d, total):
                return total + rs_v[f, k, lax.rem(chip + d, n_chips)].astype(F32)

            return lax.fori_loop(1, n_chips, add, own)

        gather_pass(FD)
        gather_pass(FC)
        gather_wait(FD)
        gather_wait(FC)
        x_in.wait_recv()

        for k in (0, 1):
            def hidden(r, k=k):
                pre = mm(x_v[r, cols(k)], w_v[FD, k]) + mm(xo_v[r, cols(k)], w_v[FC, k])
                cumul = 0.5 * (1.0 + lax.erf(pre * (1.0 / math.sqrt(2.0))))
                h_v[r, cols(k)] = (pre * cumul).astype(BF16)
                slope_v[r, cols(k)] = cumul + pre * jnp.exp(-0.5 * pre * pre) * (1.0 / math.sqrt(2.0 * math.pi))

            each_tile(hidden)

        gather_q_pass()
        gather_pass(SD)
        for k in (0, 1):
            outer(SD, k, h_v, lambda k=k: c_v[:, cols(k)])

        z_cot.wait_send()
        z_hid[1][0].start()
        z_hid[1][1].start()
        z_cot.wait_recv()
        outer(SC, 0, h_v, lambda: cq_v[...])

        fold(SD, 0)
        fold(SD, 1)
        gather_wait(SD)
        gather_q_wait()
        fold(SC, 0)

        def first_section(k):
            def grads(r):
                if k == 0:
                    from_partner = mm_nt(cq_v[r, :], scq_v[...])
                else:
                    from_partner = bs_in[r, :].astype(F32)
                total = mm_nt(c_v[r, cols(k)], w_v[SD, k]) + from_partner
                pre_grad = (total * slope_v[r, cols(k)]).astype(BF16)
                pg_v[r, cols(k)] = pre_grad
                bf_out[r, cols(k)] = mm_nt(pre_grad, w_v[FC, k]).astype(BF16)

            each_tile(grads)
            x_back[k].start()
            outer(FD, k, x_v, lambda: pg_v[:, cols(k)])
            outer(FC, k, xo_v, lambda: pg_v[:, cols(k)])
            fold(FD, k)
            fold(FC, k)

        first_section(0)
        z_back.wait_send()
        z_hid[0][0].start()
        z_hid[0][1].start()
        z_back.wait_recv()
        first_section(1)

        gq_out[...] = reduced(SC, 0).astype(BF16)
        z_grad.start()

        stores = []

        def store(src, dst):
            copy = pltpu.make_async_copy(src, dst, st_sem.at[len(stores)])
            copy.start()
            stores.append(copy)

        for k in (0, 1):
            x_back[k].wait_recv()

            def input_grad(r, k=k):
                total = mm_nt(pg_v[r, cols(k)], w_v[FD, k]) + bf_in[r, cols(k)].astype(F32)
                ig_v[r, cols(k)] = total.astype(BF16)

            each_tile(input_grad)
        store(ig_v, ig_hbm)


        def own_part(r):
            acc_v[r, :] = mm(h_v[r, cols(0)], w_v[SD, 0])

        each_tile(own_part)
        for f, g_hbm in ((SD, gsd_hbm), (FD, gfd_hbm), (FC, gfc_hbm)):
            for k in (0, 1):
                grad_v[f, k] = reduced(f, k)
            store(grad_v.at[f], g_hbm)

        z_hid[1][0].wait_recv()
        z_hid[1][1].wait_recv()
        outer(SC, 1, ho_v, lambda: c_v[:, cols(1)])

        def output(r):
            total = mm(h_v[r, cols(1)], w_v[SD, 1]) + mm(ho_v[r, cols(1)], w_v[SC, 1])
            out_v[r, cols(1)] = total.astype(BF16)

        fold(SC, 1)
        each_tile(output)
        store(out_v.at[:, cols(1)], out_hbm.at[:, cols(1)])
        z_grad.wait_recv()
        grad_v[SC, 0] = gq_in[...].astype(F32)
        grad_v[SC, 1] = reduced(SC, 1)
        store(grad_v.at[SC], gsc_hbm)
        for i, r in enumerate(halves):
            z_hid[0][i].wait_recv()
            out_v[r, cols(0)] = (acc_v[r, :] + mm(ho_v[r, cols(0)], w_v[SC, 0])).astype(BF16)
        store(out_v.at[:, cols(0)], out_hbm.at[:, cols(0)])

        for f in range(4):
            each_peer(lambda d, f=f: gather(f, dp, peer(d)).wait_send())
            each_peer(lambda d, f=f: pass_on(f, peer(d)).wait_send(), first=0)
            for k in (0, 1):
                each_peer(lambda d, f=f, k=k: scatter(f, k, dp, peer(d)).wait_send())
                each_peer(lambda d, f=f, k=k: pair(f, k, peer_twin(d)).wait_send(), first=0)
        each_peer(lambda d: gather_q(dp, peer(d)).wait_send())
        each_peer(lambda d: pass_on_q(peer(d)).wait_send(), first=0)
        for copy in (z_shard, *z_hid[0], *z_hid[1], z_grad, x_in, *x_back):
            copy.wait_send()
        for copy in stores:
            copy.wait()

    wide = (rows, 2 * width)
    dma = pltpu.SemaphoreType.DMA
    scratch = [
        pltpu.VMEM(wide, BF16),
        pltpu.VMEM(wide, BF16),
        pltpu.VMEM((4, 2, width, width), BF16),
        pltpu.VMEM((width, width), BF16),
        pltpu.VMEM(wide, BF16),
        pltpu.VMEM((rows, width), BF16),
        pltpu.VMEM((rows, width), BF16),
        pltpu.VMEM((rows, width), BF16),
        pltpu.VMEM(wide, F32),
        pltpu.VMEM(wide, BF16),
        pltpu.VMEM(wide, BF16),
        pltpu.VMEM(wide, BF16),
        pltpu.VMEM(wide, BF16),
        pltpu.VMEM(wide, BF16),
        pltpu.VMEM((4, 2, width, width), BF16),
        pltpu.VMEM((4, 2, n_chips, shard, width), BF16),
        pltpu.VMEM((4, 2, n_chips, shard, width), BF16),
        pltpu.VMEM(wide, BF16),
        pltpu.VMEM(wide, BF16),
        pltpu.VMEM((4, 2, shard, width), F32),
        pltpu.VMEM((rows, width), F32),
        pltpu.VMEM((shard, width), BF16),
        pltpu.VMEM((shard, width), BF16),
        dma((6,)),
        dma((4, n_dp)),
        dma((4, n_dp)),
        dma((n_dp,)),
        dma((n_dp,)),
        dma((10,)),
        dma((10,)),
        dma((3,)),
        dma((3,)),
        dma((4, 2, n_chips)),
        dma((4, 2, n_chips)),
        dma((4, n_dp)),
        dma((n_dp,)),
        dma((4, 2, n_chips)),
        dma((4, 2, n_chips)),
        dma((7,)),
    ]
    return kernel, scratch


def hand_over(*refs):
    sources, targets, held, load_sem, store_sem = refs[:6], refs[6:12], refs[12:18], refs[18], refs[19]
    loads = [pltpu.make_async_copy(sources[i], held[i], load_sem.at[i]) for i in range(6)]
    stores = [pltpu.make_async_copy(held[i], targets[i], store_sem.at[i]) for i in range(6)]
    for load in loads:
        load.start()
    for load, store in zip(loads, stores):
        load.wait()
        store.start()
    for store in stores:
        store.wait()


def solution(mesh):
    n_dp, n_mp = mesh.shape["dp"], mesh.shape["mp"]

    def local(*args):
        rows, two_width = args[0].shape
        shard, width = args[2].shape[1:]
        kernel, scratch = make_kernel(n_dp, n_mp, rows, width, shard)
        act = jax.ShapeDtypeStruct((rows, two_width), BF16)
        grad = jax.ShapeDtypeStruct((2, shard, width), F32)
        hbm = pl.BlockSpec(memory_space=pl.ANY)
        shapes = (act, act, grad, grad, grad, grad)
        results = pl.pallas_call(
            kernel,
            out_shape=shapes,
            in_specs=[hbm] * 6,
            out_specs=[hbm] * 6,
            scratch_shapes=scratch,
            compiler_params=pltpu.CompilerParams(
                collective_id=0, has_side_effects=True, vmem_limit_bytes=60 * 1024 * 1024
            ),
            name="butterfly",
        )(*args)
        return pl.pallas_call(
            hand_over,
            out_shape=shapes,
            in_specs=[hbm] * 6,
            out_specs=[hbm] * 6,
            scratch_shapes=[pltpu.VMEM(x.shape, x.dtype) for x in shapes] + [pltpu.SemaphoreType.DMA((6,))] * 2,
            compiler_params=pltpu.CompilerParams(vmem_limit_bytes=58 * 1024 * 1024),
            name="hand_over",
        )(*results)

    tokens = P("dp", "mp")
    blocks = P("mp", "dp", None)
    specs = (tokens, tokens, blocks, blocks, blocks, blocks)
    return jax.shard_map(local, mesh=mesh, in_specs=specs, out_specs=specs, check_vma=False)
```

```python
import math

import jax
import jax.numpy as jnp
from jax import lax
from jax.experimental import pallas as pl
from jax.experimental.pallas import tpu as pltpu
from jax.sharding import PartitionSpec as P

MESH = pl.DeviceIdType.MESH
BF16 = jnp.bfloat16
F32 = jnp.float32
FD, FC, SD, SC = range(4)


def mm(left, right):
    return lax.dot_general(left, right, (((1,), (0,)), ((), ())), preferred_element_type=F32)


def mm_nt(left, right):
    return lax.dot_general(left, right, (((1,), (1,)), ((), ())), preferred_element_type=F32)


def mm_tn(left, right):
    return lax.dot_general(left, right, (((0,), (0,)), ((), ())), preferred_element_type=F32)


def make_kernel(n_dp, n_mp, rows, width, shard):
    tile = min(128, rows)
    n_tiles = rows // tile
    n_chips = n_dp // 2
    col_tile = min(256, width)
    n_cols = width // col_tile
    tile_chips = col_tile // (2 * shard)

    def kernel(
        x_hbm, c_hbm, fd_hbm, fc_hbm, sd_hbm, sc_hbm,
        out_hbm, ig_hbm, gfd_hbm, gfc_hbm, gsd_hbm, gsc_hbm,
        x_v, c_v, w_v, scq_v, xo_v, cq_v, bs_out, bs_in, slope_v, h_v, ho_v, pg_v, bf_out, bf_in,
        part_v, rs_v, pair_v, out_v, ig_v, grad_v, acc_v, gq_out, gq_in,
        loc_sem, ag_send, ag_recv, tw_send, tw_recv, z_send, z_recv, xs_send, xs_recv,
        rs_send, rs_recv, pr_send, pr_recv, st_sem,
    ):
        dp = lax.axis_index("dp")
        mp = lax.axis_index("mp")
        zp = lax.rem(mp + n_mp // 2, n_mp)
        xp = mp + 1 - 2 * lax.rem(mp, 2)
        to_z = {"mp": zp}
        to_x = {"mp": xp}

        chip = dp // 2
        core = lax.rem(dp, 2)
        twin = dp + 1 - 2 * core
        to_twin = {"dp": twin}

        def peer(step):
            return 2 * lax.rem(chip + step, n_chips) + core

        def cols(k):
            return pl.ds(k * width, width)

        def remote(src, dst, ssem, rsem, device):
            return pltpu.make_async_remote_copy(
                src_ref=src, dst_ref=dst, send_sem=ssem, recv_sem=rsem, device_id=device, device_id_type=MESH
            )

        def each_peer(body):
            def step(d, carry):
                body(d)
                return carry

            lax.fori_loop(1, n_chips, step, 0)

        def each_tile(body):
            def step(t, carry):
                body(pl.ds(pl.multiple_of(t * tile, tile), tile))
                return carry

            lax.fori_loop(0, n_tiles, step, 0)

        shards = (fd_hbm, fc_hbm, sd_hbm, sc_hbm)
        load_w = [
            pltpu.make_async_copy(shards[f], w_v.at[f, :, dp // 2, lax.rem(dp, 2)], loc_sem.at[f]) for f in range(4)
        ]
        load_c = pltpu.make_async_copy(c_hbm, c_v, loc_sem.at[4])
        load_x = pltpu.make_async_copy(x_hbm, x_v, loc_sem.at[5])
        for load in (load_w[SC], load_c, load_x, load_w[FD], load_w[FC], load_w[SD]):
            load.start()

        barrier = pltpu.get_barrier_semaphore()
        pl.semaphore_signal(barrier, inc=1, device_id=to_z, device_id_type=MESH)
        pl.semaphore_signal(barrier, inc=1, device_id=to_x, device_id_type=MESH)
        pl.semaphore_signal(barrier, inc=1, device_id=to_twin, device_id_type=MESH)
        each_peer(lambda d: pl.semaphore_signal(barrier, inc=1, device_id={"dp": peer(d)}, device_id_type=MESH))
        pl.semaphore_wait(barrier, n_chips + 2)

        def weight(f, k):
            return w_v[f, k].reshape(width, width)

        def gather(f, target):
            view = w_v.at[f, :, chip, core]
            return remote(view, view, ag_send.at[0], ag_recv.at[f], {"dp": target})

        def gather_q(target):
            view = scq_v.at[chip, core]
            return remote(view, view, ag_send.at[1], ag_recv.at[4], {"dp": target})

        def others(view, ssem, rsem):
            return remote(view, view, ssem, rsem, to_twin)

        def gather_start(f):
            each_peer(lambda d: gather(f, peer(d)).start())

        def pass_on(f):
            view = w_v.at[f, :, :, core]
            return others(view, tw_send.at[f], tw_recv.at[f])

        def pass_on_q():
            view = scq_v.at[:, core]
            return others(view, tw_send.at[4], tw_recv.at[4])

        def gather_pass(f):
            others(w_v.at[f, :, pl.ds(0, n_chips - 1), core], ag_send.at[0], ag_recv.at[f]).wait_recv()
            pass_on(f).start()

        def gather_q_pass():
            others(scq_v.at[pl.ds(0, n_chips - 1), core], ag_send.at[1], ag_recv.at[4]).wait_recv()
            pass_on_q().start()

        def gather_wait(f):
            pass_on(f).wait_recv()

        z_shard = remote(
            w_v.at[SC, 0, chip, core], scq_v.at[chip, core], z_send.at[0], z_recv.at[0], to_z
        )
        z_cot = remote(c_v.at[:, cols(0)], cq_v, z_send.at[1], z_recv.at[1], to_z)
        z_back = remote(bs_out, bs_in, z_send.at[2], z_recv.at[2], to_z)
        halves = [pl.ds(i * (rows // 2), rows // 2) for i in (0, 1)]
        z_hid = [
            [
                remote(h_v.at[r, cols(k)], ho_v.at[r, cols(k)], z_send.at[6 + 2 * k + i], z_recv.at[6 + 2 * k + i], to_z)
                for i, r in enumerate(halves)
            ]
            for k in (0, 1)
        ]
        z_grad = remote(gq_out, gq_in, z_send.at[5], z_recv.at[5], to_z)
        x_in = remote(x_v, xo_v, xs_send.at[0], xs_recv.at[0], to_x)
        x_back = [
            remote(bf_out.at[:, cols(k)], bf_in.at[:, cols(k)], xs_send.at[1 + k], xs_recv.at[1 + k], to_x)
            for k in (0, 1)
        ]

        load_w[SC].wait()
        z_shard.start()
        load_c.wait()
        z_cot.start()
        gather_start(SC)
        load_x.wait()
        x_in.start()
        load_w[FD].wait()
        gather_start(FD)
        load_w[FC].wait()
        gather_start(FC)
        z_shard.wait_recv()
        each_peer(lambda d: gather_q(peer(d)).start())
        load_w[SD].wait()
        gather_start(SD)

        gather_pass(SC)
        gather_wait(SC)

        def back_second(r):
            bs_out[r, :] = mm_nt(c_v[r, cols(1)], weight(SC, 1)).astype(BF16)

        each_tile(back_second)
        z_back.start()

        def pair(f, k):
            return remote(
                part_v.at[f, k, :, 1 - core], pair_v.at[f, k], pr_send.at[f, k], pr_recv.at[f, k], to_twin
            )

        def scatter(f, k, d):
            target = lax.rem(chip + d, n_chips)
            return remote(
                part_v.at[f, k, target, core], rs_v.at[f, k, chip], rs_send.at[f, k], rs_recv.at[f, k], {"dp": peer(d)}
            )

        def fold(f, k):
            pair(f, k).wait_recv()
            both = part_v[f, k, :, core].astype(F32) + pair_v[f, k].astype(F32)
            part_v[f, k, :, core] = both.astype(BF16)
            each_peer(lambda d: scatter(f, k, d).start())

        def most(f, k):
            view = rs_v.at[f, k, pl.ds(0, n_chips - 1)]
            return others(view, rs_send.at[f, k], rs_recv.at[f, k])

        def outer(f, k, left, right):
            def step(j, carry):
                lb = pl.ds(pl.multiple_of(k * width + j * col_tile, col_tile), col_tile)
                product = mm_tn(left[:, lb], right()).astype(BF16)
                part_v[f, k, pl.ds(j * tile_chips, tile_chips)] = product.reshape(tile_chips, 2, shard, width)
                return carry

            lax.fori_loop(0, n_cols, step, 0)
            pair(f, k).start()

        def reduced(f, k):
            most(f, k).wait_recv()
            own = part_v[f, k, chip, core].astype(F32)

            def add(d, total):
                return total + rs_v[f, k, lax.rem(chip + d, n_chips)].astype(F32)

            return lax.fori_loop(1, n_chips, add, own)

        gather_pass(FD)
        gather_pass(FC)
        gather_wait(FD)
        gather_wait(FC)
        x_in.wait_recv()

        for k in (0, 1):
            def hidden(r, k=k):
                pre = mm(x_v[r, cols(k)], weight(FD, k)) + mm(xo_v[r, cols(k)], weight(FC, k))
                cumul = 0.5 * (1.0 + lax.erf(pre * (1.0 / math.sqrt(2.0))))
                h_v[r, cols(k)] = (pre * cumul).astype(BF16)
                slope_v[r, cols(k)] = cumul + pre * jnp.exp(-0.5 * pre * pre) * (1.0 / math.sqrt(2.0 * math.pi))

            each_tile(hidden)

        gather_q_pass()
        gather_pass(SD)
        for k in (0, 1):
            outer(SD, k, h_v, lambda k=k: c_v[:, cols(k)])

        z_cot.wait_send()
        z_hid[1][0].start()
        z_hid[1][1].start()
        z_cot.wait_recv()
        outer(SC, 0, h_v, lambda: cq_v[...])

        fold(SD, 0)
        fold(SD, 1)
        gather_wait(SD)
        pass_on_q().wait_recv()
        fold(SC, 0)

        def first_section(k):
            def grads(r):
                if k == 0:
                    from_partner = mm_nt(cq_v[r, :], scq_v[...].reshape(width, width))
                else:
                    from_partner = bs_in[r, :].astype(F32)
                total = mm_nt(c_v[r, cols(k)], weight(SD, k)) + from_partner
                pre_grad = (total * slope_v[r, cols(k)]).astype(BF16)
                pg_v[r, cols(k)] = pre_grad
                bf_out[r, cols(k)] = mm_nt(pre_grad, weight(FC, k)).astype(BF16)

            each_tile(grads)
            x_back[k].start()
            outer(FD, k, x_v, lambda: pg_v[:, cols(k)])
            outer(FC, k, xo_v, lambda: pg_v[:, cols(k)])
            fold(FD, k)
            fold(FC, k)

        first_section(0)
        z_back.wait_recv()
        first_section(1)
        z_hid[1][0].wait_send()
        z_hid[0][0].start()

        gq_out[...] = reduced(SC, 0).astype(BF16)
        z_grad.start()

        stores = []

        def store(src, dst):
            copy = pltpu.make_async_copy(src, dst, st_sem.at[len(stores)])
            copy.start()
            stores.append(copy)

        for k in (0, 1):
            x_back[k].wait_recv()

            def input_grad(r, k=k):
                total = mm_nt(pg_v[r, cols(k)], weight(FD, k)) + bf_in[r, cols(k)].astype(F32)
                ig_v[r, cols(k)] = total.astype(BF16)

            each_tile(input_grad)
        store(ig_v, ig_hbm)


        z_hid[1][1].wait_send()
        z_hid[0][1].start()

        def own_part(r):
            acc_v[r, :] = mm(h_v[r, cols(0)], weight(SD, 0))

        each_tile(own_part)
        for f, g_hbm in ((SD, gsd_hbm), (FD, gfd_hbm), (FC, gfc_hbm)):
            for k in (0, 1):
                grad_v[f, k] = reduced(f, k)
            store(grad_v.at[f], g_hbm)

        z_hid[1][0].wait_recv()
        z_hid[1][1].wait_recv()
        outer(SC, 1, ho_v, lambda: c_v[:, cols(1)])

        def output(r):
            total = mm(h_v[r, cols(1)], weight(SD, 1)) + mm(ho_v[r, cols(1)], weight(SC, 1))
            out_v[r, cols(1)] = total.astype(BF16)

        fold(SC, 1)
        each_tile(output)
        store(out_v.at[:, cols(1)], out_hbm.at[:, cols(1)])
        z_grad.wait_recv()
        grad_v[SC, 0] = gq_in[...].astype(F32)
        grad_v[SC, 1] = reduced(SC, 1)
        store(grad_v.at[SC], gsc_hbm)
        for i, r in enumerate(halves):
            z_hid[0][i].wait_recv()
            out_v[r, cols(0)] = (acc_v[r, :] + mm(ho_v[r, cols(0)], weight(SC, 0))).astype(BF16)
        store(out_v.at[:, cols(0)], out_hbm.at[:, cols(0)])

        others(w_v.at[:, :, pl.ds(0, n_chips - 1), core], ag_send.at[0], ag_recv.at[0]).wait_send()
        others(scq_v.at[pl.ds(0, n_chips - 1), core], ag_send.at[1], ag_recv.at[4]).wait_send()
        pass_on_q().wait_send()
        for f in range(4):
            pass_on(f).wait_send()
            for k in (0, 1):
                pair(f, k).wait_send()
                most(f, k).wait_send()
        for copy in (z_shard, z_back, *z_hid[0], z_grad, x_in, *x_back):
            copy.wait_send()
        for copy in stores:
            copy.wait()

    wide = (rows, 2 * width)
    dma = pltpu.SemaphoreType.DMA
    scratch = [
        pltpu.VMEM(wide, BF16),
        pltpu.VMEM(wide, BF16),
        pltpu.VMEM((4, 2, n_dp // 2, 2, shard, width), BF16),
        pltpu.VMEM((n_dp // 2, 2, shard, width), BF16),
        pltpu.VMEM(wide, BF16),
        pltpu.VMEM((rows, width), BF16),
        pltpu.VMEM((rows, width), BF16),
        pltpu.VMEM((rows, width), BF16),
        pltpu.VMEM(wide, F32),
        pltpu.VMEM(wide, BF16),
        pltpu.VMEM(wide, BF16),
        pltpu.VMEM(wide, BF16),
        pltpu.VMEM(wide, BF16),
        pltpu.VMEM(wide, BF16),
        pltpu.VMEM((4, 2, n_dp // 2, 2, shard, width), BF16),
        pltpu.VMEM((4, 2, n_dp // 2, shard, width), BF16),
        pltpu.VMEM((4, 2, n_dp // 2, shard, width), BF16),
        pltpu.VMEM(wide, BF16),
        pltpu.VMEM(wide, BF16),
        pltpu.VMEM((4, 2, shard, width), F32),
        pltpu.VMEM((rows, width), F32),
        pltpu.VMEM((shard, width), BF16),
        pltpu.VMEM((shard, width), BF16),
        dma((6,)),
        dma((2,)),
        dma((5,)),
        dma((5,)),
        dma((5,)),
        dma((10,)),
        dma((10,)),
        dma((3,)),
        dma((3,)),
        dma((4, 2)),
        dma((4, 2)),
        dma((4, 2)),
        dma((4, 2)),
        dma((7,)),
    ]
    return kernel, scratch


def hand_over(*refs):
    sources, targets, held, load_sem, store_sem = refs[:6], refs[6:12], refs[12:18], refs[18], refs[19]
    loads = [pltpu.make_async_copy(sources[i], held[i], load_sem.at[i]) for i in range(6)]
    stores = [pltpu.make_async_copy(held[i], targets[i], store_sem.at[i]) for i in range(6)]
    for load in loads:
        load.start()
    for load, store in zip(loads, stores):
        load.wait()
        store.start()
    for store in stores:
        store.wait()


def solution(mesh):
    n_dp, n_mp = mesh.shape["dp"], mesh.shape["mp"]

    def local(*args):
        rows, two_width = args[0].shape
        shard, width = args[2].shape[1:]
        kernel, scratch = make_kernel(n_dp, n_mp, rows, width, shard)
        act = jax.ShapeDtypeStruct((rows, two_width), BF16)
        grad = jax.ShapeDtypeStruct((2, shard, width), F32)
        hbm = pl.BlockSpec(memory_space=pl.ANY)
        shapes = (act, act, grad, grad, grad, grad)
        results = pl.pallas_call(
            kernel,
            out_shape=shapes,
            in_specs=[hbm] * 6,
            out_specs=[hbm] * 6,
            scratch_shapes=scratch,
            compiler_params=pltpu.CompilerParams(
                collective_id=0, has_side_effects=True, vmem_limit_bytes=60 * 1024 * 1024
            ),
            name="butterfly",
        )(*args)
        return pl.pallas_call(
            hand_over,
            out_shape=shapes,
            in_specs=[hbm] * 6,
            out_specs=[hbm] * 6,
            scratch_shapes=[pltpu.VMEM(x.shape, x.dtype) for x in shapes] + [pltpu.SemaphoreType.DMA((6,))] * 2,
            compiler_params=pltpu.CompilerParams(vmem_limit_bytes=58 * 1024 * 1024),
            name="hand_over",
        )(*results)

    tokens = P("dp", "mp")
    blocks = P("mp", "dp", None)
    specs = (tokens, tokens, blocks, blocks, blocks, blocks)
    return jax.shard_map(local, mesh=mesh, in_specs=specs, out_specs=specs, check_vma=False)
```

```python
import math

import jax
import jax.numpy as jnp
from jax import lax
from jax.experimental import pallas as pl
from jax.experimental.pallas import tpu as pltpu
from jax.sharding import PartitionSpec as P

MESH = pl.DeviceIdType.MESH
BF16 = jnp.bfloat16
F32 = jnp.float32
FD, FC, SD, SC = range(4)


def mm(left, right):
    return lax.dot_general(left, right, (((1,), (0,)), ((), ())), preferred_element_type=F32)


def mm_nt(left, right):
    return lax.dot_general(left, right, (((1,), (1,)), ((), ())), preferred_element_type=F32)


def mm_tn(left, right):
    return lax.dot_general(left, right, (((0,), (0,)), ((), ())), preferred_element_type=F32)


def make_kernel(n_dp, n_mp, rows, width, shard):
    tile = min(128, rows)
    n_tiles = rows // tile
    n_chips = n_dp // 2
    col_tile = min(256, width)
    n_cols = width // col_tile
    tile_chips = col_tile // (2 * shard)

    def kernel(
        x_hbm, c_hbm, fd_hbm, fc_hbm, sd_hbm, sc_hbm,
        out_v, ig_v, gfd_v, gfc_v, gsd_v, gsc_v,
        x_v, c_v, w_v, scq_v, xo_v, cq_v, bs_out, bs_in, slope_v, h_v, ho_v, pg_v, bf_out, bf_in,
        part_v, rs_v, pair_v, acc_v, gq_out, gq_in,
        loc_sem, ag_send, ag_recv, tw_send, tw_recv, z_send, z_recv, xs_send, xs_recv,
        rs_send, rs_recv, pr_send, pr_recv,
    ):
        dp = lax.axis_index("dp")
        mp = lax.axis_index("mp")
        zp = lax.rem(mp + n_mp // 2, n_mp)
        xp = mp + 1 - 2 * lax.rem(mp, 2)
        to_z = {"mp": zp}
        to_x = {"mp": xp}

        chip = dp // 2
        core = lax.rem(dp, 2)
        twin = dp + 1 - 2 * core
        to_twin = {"dp": twin}

        def peer(step):
            return 2 * lax.rem(chip + step, n_chips) + core

        def cols(k):
            return pl.ds(k * width, width)

        def remote(src, dst, ssem, rsem, device):
            return pltpu.make_async_remote_copy(
                src_ref=src, dst_ref=dst, send_sem=ssem, recv_sem=rsem, device_id=device, device_id_type=MESH
            )

        def each_peer(body):
            def step(d, carry):
                body(d)
                return carry

            lax.fori_loop(1, n_chips, step, 0)

        def each_tile(body):
            def step(t, carry):
                body(pl.ds(pl.multiple_of(t * tile, tile), tile))
                return carry

            lax.fori_loop(0, n_tiles, step, 0)

        shards = (fd_hbm, fc_hbm, sd_hbm, sc_hbm)
        load_w = [
            pltpu.make_async_copy(shards[f], w_v.at[f, :, dp // 2, lax.rem(dp, 2)], loc_sem.at[f]) for f in range(4)
        ]
        load_c = pltpu.make_async_copy(c_hbm, c_v, loc_sem.at[4])
        load_x = pltpu.make_async_copy(x_hbm, x_v, loc_sem.at[5])
        for load in (load_w[SC], load_c, load_x, load_w[FD], load_w[FC], load_w[SD]):
            load.start()

        barrier = pltpu.get_barrier_semaphore()
        pl.semaphore_signal(barrier, inc=1, device_id=to_z, device_id_type=MESH)
        pl.semaphore_signal(barrier, inc=1, device_id=to_x, device_id_type=MESH)
        pl.semaphore_signal(barrier, inc=1, device_id=to_twin, device_id_type=MESH)
        each_peer(lambda d: pl.semaphore_signal(barrier, inc=1, device_id={"dp": peer(d)}, device_id_type=MESH))
        pl.semaphore_wait(barrier, n_chips + 2)

        def weight(f, k):
            return w_v[f, k].reshape(width, width)

        def gather(f, target):
            view = w_v.at[f, :, chip, core]
            return remote(view, view, ag_send.at[0], ag_recv.at[f], {"dp": target})

        def gather_q(target):
            view = scq_v.at[chip, core]
            return remote(view, view, ag_send.at[1], ag_recv.at[4], {"dp": target})

        def others(view, ssem, rsem):
            return remote(view, view, ssem, rsem, to_twin)

        def gather_start(f):
            each_peer(lambda d: gather(f, peer(d)).start())

        def pass_on(f):
            view = w_v.at[f, :, :, core]
            return others(view, tw_send.at[f], tw_recv.at[f])

        def pass_on_q():
            view = scq_v.at[:, core]
            return others(view, tw_send.at[4], tw_recv.at[4])

        def gather_pass(f):
            others(w_v.at[f, :, pl.ds(0, n_chips - 1), core], ag_send.at[0], ag_recv.at[f]).wait_recv()
            pass_on(f).start()

        def gather_q_pass():
            others(scq_v.at[pl.ds(0, n_chips - 1), core], ag_send.at[1], ag_recv.at[4]).wait_recv()
            pass_on_q().start()

        def gather_wait(f):
            pass_on(f).wait_recv()

        z_shard = remote(
            w_v.at[SC, 0, chip, core], scq_v.at[chip, core], z_send.at[0], z_recv.at[0], to_z
        )
        z_cot = remote(c_v.at[:, cols(0)], cq_v, z_send.at[1], z_recv.at[1], to_z)
        z_back = remote(bs_out, bs_in, z_send.at[2], z_recv.at[2], to_z)
        halves = [pl.ds(i * (rows // 2), rows // 2) for i in (0, 1)]
        z_hid = [
            [
                remote(h_v.at[r, cols(k)], ho_v.at[r, cols(k)], z_send.at[6 + 2 * k + i], z_recv.at[6 + 2 * k + i], to_z)
                for i, r in enumerate(halves)
            ]
            for k in (0, 1)
        ]
        z_grad = remote(gq_out, gq_in, z_send.at[5], z_recv.at[5], to_z)
        x_in = remote(x_v, xo_v, xs_send.at[0], xs_recv.at[0], to_x)
        x_back = [
            remote(bf_out.at[:, cols(k)], bf_in.at[:, cols(k)], xs_send.at[1 + k], xs_recv.at[1 + k], to_x)
            for k in (0, 1)
        ]

        load_w[SC].wait()
        z_shard.start()
        load_c.wait()
        z_cot.start()
        gather_start(SC)
        load_x.wait()
        x_in.start()
        load_w[FD].wait()
        gather_start(FD)
        load_w[FC].wait()
        gather_start(FC)
        z_shard.wait_recv()
        each_peer(lambda d: gather_q(peer(d)).start())
        load_w[SD].wait()
        gather_start(SD)

        gather_pass(SC)
        gather_wait(SC)

        def back_second(r):
            bs_out[r, :] = mm_nt(c_v[r, cols(1)], weight(SC, 1)).astype(BF16)

        each_tile(back_second)
        z_back.start()

        def pair(f, k):
            return remote(
                part_v.at[f, k, :, 1 - core], pair_v.at[f, k], pr_send.at[f, k], pr_recv.at[f, k], to_twin
            )

        def scatter(f, k, d):
            target = lax.rem(chip + d, n_chips)
            return remote(
                part_v.at[f, k, target, core], rs_v.at[f, k, chip], rs_send.at[f, k], rs_recv.at[f, k], {"dp": peer(d)}
            )

        def fold(f, k):
            pair(f, k).wait_recv()
            both = part_v[f, k, :, core].astype(F32) + pair_v[f, k].astype(F32)
            part_v[f, k, :, core] = both.astype(BF16)
            each_peer(lambda d: scatter(f, k, d).start())

        def most(f, k):
            view = rs_v.at[f, k, pl.ds(0, n_chips - 1)]
            return others(view, rs_send.at[f, k], rs_recv.at[f, k])

        def outer(f, k, left, right):
            def step(j, carry):
                lb = pl.ds(pl.multiple_of(k * width + j * col_tile, col_tile), col_tile)
                product = mm_tn(left[:, lb], right()).astype(BF16)
                part_v[f, k, pl.ds(j * tile_chips, tile_chips)] = product.reshape(tile_chips, 2, shard, width)
                return carry

            lax.fori_loop(0, n_cols, step, 0)
            pair(f, k).start()

        def reduced(f, k):
            most(f, k).wait_recv()
            own = part_v[f, k, chip, core].astype(F32)

            def add(d, total):
                return total + rs_v[f, k, lax.rem(chip + d, n_chips)].astype(F32)

            return lax.fori_loop(1, n_chips, add, own)

        gather_pass(FD)
        gather_pass(FC)
        gather_wait(FD)
        gather_wait(FC)
        x_in.wait_recv()

        for k in (0, 1):
            def hidden(r, k=k):
                pre = mm(x_v[r, cols(k)], weight(FD, k)) + mm(xo_v[r, cols(k)], weight(FC, k))
                cumul = 0.5 * (1.0 + lax.erf(pre * (1.0 / math.sqrt(2.0))))
                h_v[r, cols(k)] = (pre * cumul).astype(BF16)
                slope_v[r, cols(k)] = cumul + pre * jnp.exp(-0.5 * pre * pre) * (1.0 / math.sqrt(2.0 * math.pi))

            each_tile(hidden)

        gather_q_pass()
        gather_pass(SD)
        for k in (0, 1):
            outer(SD, k, h_v, lambda k=k: c_v[:, cols(k)])

        z_cot.wait_send()
        z_hid[1][0].start()
        z_cot.wait_recv()
        outer(SC, 0, h_v, lambda: cq_v[...])

        fold(SD, 0)
        fold(SD, 1)
        gather_wait(SD)
        pass_on_q().wait_recv()
        fold(SC, 0)

        def first_section(k):
            def grads(r):
                if k == 0:
                    from_partner = mm_nt(cq_v[r, :], scq_v[...].reshape(width, width))
                else:
                    from_partner = bs_in[r, :].astype(F32)
                total = mm_nt(c_v[r, cols(k)], weight(SD, k)) + from_partner
                pre_grad = (total * slope_v[r, cols(k)]).astype(BF16)
                pg_v[r, cols(k)] = pre_grad
                bf_out[r, cols(k)] = mm_nt(pre_grad, weight(FC, k)).astype(BF16)

            each_tile(grads)
            x_back[k].start()
            outer(FD, k, x_v, lambda: pg_v[:, cols(k)])
            outer(FC, k, xo_v, lambda: pg_v[:, cols(k)])
            fold(FD, k)
            fold(FC, k)

        first_section(0)
        z_back.wait_send()
        z_hid[1][1].start()
        z_back.wait_recv()
        first_section(1)
        z_hid[1][0].wait_send()
        z_hid[0][0].start()

        gq_out[...] = reduced(SC, 0).astype(BF16)
        z_grad.start()

        z_hid[1][1].wait_send()
        z_hid[0][1].start()

        def own_part(r):
            acc_v[r, :] = mm(h_v[r, cols(0)], weight(SD, 0))

        each_tile(own_part)
        z_hid[1][0].wait_recv()
        z_hid[1][1].wait_recv()
        outer(SC, 1, ho_v, lambda: c_v[:, cols(1)])

        def output(r):
            total = mm(h_v[r, cols(1)], weight(SD, 1)) + mm(ho_v[r, cols(1)], weight(SC, 1))
            out_v[r, cols(1)] = total.astype(BF16)

        fold(SC, 1)
        each_tile(output)
        for k in (0, 1):
            x_back[k].wait_recv()

            def input_grad(r, k=k):
                total = mm_nt(pg_v[r, cols(k)], weight(FD, k)) + bf_in[r, cols(k)].astype(F32)
                ig_v[r, cols(k)] = total.astype(BF16)

            each_tile(input_grad)
        for f, g_v in ((SD, gsd_v), (FD, gfd_v), (FC, gfc_v)):
            for k in (0, 1):
                g_v[k] = reduced(f, k)

        z_grad.wait_recv()
        gsc_v[0] = gq_in[...].astype(F32)
        gsc_v[1] = reduced(SC, 1)
        for i, r in enumerate(halves):
            z_hid[0][i].wait_recv()
            out_v[r, cols(0)] = (acc_v[r, :] + mm(ho_v[r, cols(0)], weight(SC, 0))).astype(BF16)

        others(w_v.at[:, :, pl.ds(0, n_chips - 1), core], ag_send.at[0], ag_recv.at[0]).wait_send()
        others(scq_v.at[pl.ds(0, n_chips - 1), core], ag_send.at[1], ag_recv.at[4]).wait_send()
        pass_on_q().wait_send()
        for f in range(4):
            pass_on(f).wait_send()
            for k in (0, 1):
                pair(f, k).wait_send()
                most(f, k).wait_send()
        for copy in (z_shard, *z_hid[0], z_grad, x_in, *x_back):
            copy.wait_send()

    wide = (rows, 2 * width)
    dma = pltpu.SemaphoreType.DMA
    scratch = [
        pltpu.VMEM(wide, BF16),
        pltpu.VMEM(wide, BF16),
        pltpu.VMEM((4, 2, n_dp // 2, 2, shard, width), BF16),
        pltpu.VMEM((n_dp // 2, 2, shard, width), BF16),
        pltpu.VMEM(wide, BF16),
        pltpu.VMEM((rows, width), BF16),
        pltpu.VMEM((rows, width), BF16),
        pltpu.VMEM((rows, width), BF16),
        pltpu.VMEM(wide, F32),
        pltpu.VMEM(wide, BF16),
        pltpu.VMEM(wide, BF16),
        pltpu.VMEM(wide, BF16),
        pltpu.VMEM(wide, BF16),
        pltpu.VMEM(wide, BF16),
        pltpu.VMEM((4, 2, n_dp // 2, 2, shard, width), BF16),
        pltpu.VMEM((4, 2, n_dp // 2, shard, width), BF16),
        pltpu.VMEM((4, 2, n_dp // 2, shard, width), BF16),
        pltpu.VMEM((rows, width), F32),
        pltpu.VMEM((shard, width), BF16),
        pltpu.VMEM((shard, width), BF16),
        dma((6,)),
        dma((2,)),
        dma((5,)),
        dma((5,)),
        dma((5,)),
        dma((10,)),
        dma((10,)),
        dma((3,)),
        dma((3,)),
        dma((4, 2)),
        dma((4, 2)),
        dma((4, 2)),
        dma((4, 2)),
    ]
    return kernel, scratch


def hand_over(*refs):
    copies = [pltpu.make_async_copy(refs[i], refs[6 + i], refs[12].at[i]) for i in range(6)]
    for copy in copies:
        copy.start()
    for copy in copies:
        copy.wait()


def solution(mesh):
    n_dp, n_mp = mesh.shape["dp"], mesh.shape["mp"]

    def local(*args):
        rows, two_width = args[0].shape
        shard, width = args[2].shape[1:]
        kernel, scratch = make_kernel(n_dp, n_mp, rows, width, shard)
        act = jax.ShapeDtypeStruct((rows, two_width), BF16)
        grad = jax.ShapeDtypeStruct((2, shard, width), F32)
        hbm = pl.BlockSpec(memory_space=pl.ANY)
        shapes = (act, act, grad, grad, grad, grad)
        vmem = pl.BlockSpec(memory_space=pltpu.VMEM)
        args = [pltpu.with_memory_space_constraint(a, pltpu.HBM) for a in args]
        results = pl.pallas_call(
            kernel,
            out_shape=shapes,
            in_specs=[hbm] * 6,
            out_specs=[vmem] * 6,
            scratch_shapes=scratch,
            compiler_params=pltpu.CompilerParams(
                collective_id=0, has_side_effects=True, vmem_limit_bytes=48 * 1024 * 1024
            ),
            name="butterfly",
        )(*args)
        return pl.pallas_call(
            hand_over,
            out_shape=shapes,
            in_specs=[vmem] * 6,
            out_specs=[pl.BlockSpec(memory_space=pltpu.HBM)] * 6,
            scratch_shapes=[pltpu.SemaphoreType.DMA((6,))],
            compiler_params=pltpu.CompilerParams(vmem_limit_bytes=16 * 1024 * 1024),
            name="hand_over",
        )(*results)

    tokens = P("dp", "mp")
    blocks = P("mp", "dp", None)
    specs = (tokens, tokens, blocks, blocks, blocks, blocks)
    return jax.shard_map(local, mesh=mesh, in_specs=specs, out_specs=specs, check_vma=False)
```

```python
import math

import jax
import jax.numpy as jnp
from jax import lax
from jax.experimental import pallas as pl
from jax.experimental.pallas import tpu as pltpu
from jax.sharding import PartitionSpec as P

MESH = pl.DeviceIdType.MESH
BF16 = jnp.bfloat16
F32 = jnp.float32
FD, FC, SD, SC = range(4)


def mm(left, right):
    return lax.dot_general(left, right, (((1,), (0,)), ((), ())), preferred_element_type=F32)


def mm_nt(left, right):
    return lax.dot_general(left, right, (((1,), (1,)), ((), ())), preferred_element_type=F32)


def mm_tn(left, right):
    return lax.dot_general(left, right, (((0,), (0,)), ((), ())), preferred_element_type=F32)


def make_kernel(n_dp, n_mp, rows, width, shard):
    tile = min(128, rows)
    n_tiles = rows // tile
    n_chips = n_dp // 2
    col_tile = min(256, width)
    n_cols = width // col_tile
    tile_chips = col_tile // (2 * shard)

    def kernel(
        x_hbm, c_hbm, fd_hbm, fc_hbm, sd_hbm, sc_hbm,
        out_v, ig_v, gfd_v, gfc_v, gsd_v, gsc_v,
        x_v, c_v, w_v, scq_v, xo_v, cq_v, bs_out, bs_in, slope_v, h_v, ho_v, pg_v, bf_out, bf_in,
        part_v, rs_v, pair_v, acc_v, gq_out, gq_in,
        loc_sem, ag_send, ag_recv, tw_send, tw_recv, z_send, z_recv, xs_send, xs_recv,
        rs_send, rs_recv, pr_send, pr_recv,
    ):
        dp = lax.axis_index("dp")
        mp = lax.axis_index("mp")
        zp = lax.rem(mp + n_mp // 2, n_mp)
        xp = mp + 1 - 2 * lax.rem(mp, 2)
        to_z = {"mp": zp}
        to_x = {"mp": xp}

        chip = dp // 2
        core = lax.rem(dp, 2)
        twin = dp + 1 - 2 * core
        to_twin = {"dp": twin}

        def peer(step):
            return 2 * lax.rem(chip + step, n_chips) + core

        def cols(k):
            return pl.ds(k * width, width)

        def remote(src, dst, ssem, rsem, device):
            return pltpu.make_async_remote_copy(
                src_ref=src, dst_ref=dst, send_sem=ssem, recv_sem=rsem, device_id=device, device_id_type=MESH
            )

        def each_peer(body):
            def step(d, carry):
                body(d)
                return carry

            lax.fori_loop(1, n_chips, step, 0)

        def each_tile(body):
            def step(t, carry):
                body(pl.ds(pl.multiple_of(t * tile, tile), tile))
                return carry

            lax.fori_loop(0, n_tiles, step, 0)

        shards = (fd_hbm, fc_hbm, sd_hbm, sc_hbm)
        load_w = [
            pltpu.make_async_copy(shards[f], w_v.at[f, :, dp // 2, lax.rem(dp, 2)], loc_sem.at[f]) for f in range(4)
        ]
        load_c = pltpu.make_async_copy(c_hbm, c_v, loc_sem.at[4])
        load_x = pltpu.make_async_copy(x_hbm, x_v, loc_sem.at[5])
        barrier = pltpu.get_barrier_semaphore()
        pl.semaphore_signal(barrier, inc=1, device_id=to_z, device_id_type=MESH)
        pl.semaphore_signal(barrier, inc=1, device_id=to_x, device_id_type=MESH)
        pl.semaphore_signal(barrier, inc=1, device_id=to_twin, device_id_type=MESH)
        each_peer(lambda d: pl.semaphore_signal(barrier, inc=1, device_id={"dp": peer(d)}, device_id_type=MESH))
        for load in (load_w[SC], load_c, load_x, load_w[FD], load_w[FC], load_w[SD]):
            load.start()
        pl.semaphore_wait(barrier, n_chips + 2)

        def weight(f, k):
            return w_v[f, k].reshape(width, width)

        def gather(f, target):
            view = w_v.at[f, :, chip, core]
            return remote(view, view, ag_send.at[0], ag_recv.at[f], {"dp": target})

        def gather_q(target):
            view = scq_v.at[chip, core]
            return remote(view, view, ag_send.at[1], ag_recv.at[4], {"dp": target})

        def others(view, ssem, rsem):
            return remote(view, view, ssem, rsem, to_twin)

        def gather_start(f):
            each_peer(lambda d: gather(f, peer(d)).start())

        def pass_on(f):
            view = w_v.at[f, :, :, core]
            return others(view, tw_send.at[0], tw_recv.at[f])

        def pass_on_q():
            view = scq_v.at[:, core]
            return others(view, tw_send.at[1], tw_recv.at[4])

        def gather_pass(f):
            others(w_v.at[f, :, pl.ds(0, n_chips - 1), core], ag_send.at[0], ag_recv.at[f]).wait_recv()
            pass_on(f).start()

        def gather_q_pass():
            others(scq_v.at[pl.ds(0, n_chips - 1), core], ag_send.at[1], ag_recv.at[4]).wait_recv()
            pass_on_q().start()

        def gather_wait(f):
            pass_on(f).wait_recv()

        z_shard = remote(
            w_v.at[SC, 0, chip, core], scq_v.at[chip, core], z_send.at[0], z_recv.at[0], to_z
        )
        z_cot = remote(c_v.at[:, cols(0)], cq_v, z_send.at[1], z_recv.at[1], to_z)
        z_back = remote(bs_out, bs_in, z_send.at[2], z_recv.at[2], to_z)
        halves = [pl.ds(i * (rows // 2), rows // 2) for i in (0, 1)]
        z_hid = [
            [
                remote(h_v.at[r, cols(k)], ho_v.at[r, cols(k)], z_send.at[6 + 2 * k + i], z_recv.at[6 + 2 * k + i], to_z)
                for i, r in enumerate(halves)
            ]
            for k in (0, 1)
        ]
        z_grad = remote(gq_out, gq_in, z_send.at[5], z_recv.at[5], to_z)
        x_in = remote(x_v, xo_v, xs_send.at[0], xs_recv.at[0], to_x)
        x_back = [
            remote(bf_out.at[:, cols(k)], bf_in.at[:, cols(k)], xs_send.at[1 + k], xs_recv.at[1 + k], to_x)
            for k in (0, 1)
        ]

        load_w[SC].wait()
        z_shard.start()
        load_c.wait()
        z_cot.start()
        gather_start(SC)
        load_x.wait()
        x_in.start()
        load_w[FD].wait()
        gather_start(FD)
        load_w[FC].wait()
        gather_start(FC)
        z_shard.wait_recv()
        each_peer(lambda d: gather_q(peer(d)).start())
        load_w[SD].wait()
        gather_start(SD)

        gather_pass(SC)
        gather_wait(SC)

        def back_second(r):
            bs_out[r, :] = mm_nt(c_v[r, cols(1)], weight(SC, 1)).astype(BF16)

        each_tile(back_second)
        z_back.start()

        def pair(f, k):
            return remote(
                part_v.at[f, k, :, 1 - core], pair_v.at[f, k], pr_send.at[0], pr_recv.at[f, k], to_twin
            )

        def scatter(f, k, d):
            target = lax.rem(chip + d, n_chips)
            return remote(
                part_v.at[f, k, target, core], rs_v.at[f, k, chip], rs_send.at[0], rs_recv.at[f, k], {"dp": peer(d)}
            )

        def fold(f, k):
            pair(f, k).wait_recv()
            both = part_v[f, k, :, core].astype(F32) + pair_v[f, k].astype(F32)
            part_v[f, k, :, core] = both.astype(BF16)
            each_peer(lambda d: scatter(f, k, d).start())

        def most(f, k):
            view = rs_v.at[f, k, pl.ds(0, n_chips - 1)]
            return others(view, rs_send.at[0], rs_recv.at[f, k])

        def outer(f, k, left, right):
            def step(j, carry):
                lb = pl.ds(pl.multiple_of(k * width + j * col_tile, col_tile), col_tile)
                product = mm_tn(left[:, lb], right()).astype(BF16)
                part_v[f, k, pl.ds(j * tile_chips, tile_chips)] = product.reshape(tile_chips, 2, shard, width)
                return carry

            lax.fori_loop(0, n_cols, step, 0)
            pair(f, k).start()

        def reduced(f, k):
            most(f, k).wait_recv()
            own = part_v[f, k, chip, core].astype(F32)

            def add(d, total):
                return total + rs_v[f, k, lax.rem(chip + d, n_chips)].astype(F32)

            return lax.fori_loop(1, n_chips, add, own)

        gather_pass(FD)
        gather_pass(FC)
        gather_wait(FD)
        gather_wait(FC)
        x_in.wait_recv()

        for k in (0, 1):
            def hidden(r, k=k):
                pre = mm(x_v[r, cols(k)], weight(FD, k)) + mm(xo_v[r, cols(k)], weight(FC, k))
                cumul = 0.5 * (1.0 + lax.erf(pre * (1.0 / math.sqrt(2.0))))
                h_v[r, cols(k)] = (pre * cumul).astype(BF16)
                slope_v[r, cols(k)] = cumul + pre * jnp.exp(-0.5 * pre * pre) * (1.0 / math.sqrt(2.0 * math.pi))

            each_tile(hidden)

        gather_q_pass()
        gather_pass(SD)
        for k in (0, 1):
            outer(SD, k, h_v, lambda k=k: c_v[:, cols(k)])

        z_cot.wait_send()
        z_hid[1][0].start()
        z_cot.wait_recv()
        outer(SC, 0, h_v, lambda: cq_v[...])

        fold(SD, 0)
        fold(SD, 1)
        gather_wait(SD)
        pass_on_q().wait_recv()
        fold(SC, 0)

        def first_section(k):
            def grads(r):
                if k == 0:
                    from_partner = mm_nt(cq_v[r, :], scq_v[...].reshape(width, width))
                else:
                    from_partner = bs_in[r, :].astype(F32)
                total = mm_nt(c_v[r, cols(k)], weight(SD, k)) + from_partner
                pre_grad = (total * slope_v[r, cols(k)]).astype(BF16)
                pg_v[r, cols(k)] = pre_grad
                bf_out[r, cols(k)] = mm_nt(pre_grad, weight(FC, k)).astype(BF16)

            each_tile(grads)
            x_back[k].start()
            outer(FD, k, x_v, lambda: pg_v[:, cols(k)])
            outer(FC, k, xo_v, lambda: pg_v[:, cols(k)])
            fold(FD, k)
            fold(FC, k)

        first_section(0)
        z_back.wait_send()
        z_hid[1][1].start()
        z_back.wait_recv()
        first_section(1)
        z_hid[1][0].wait_send()
        z_hid[0][0].start()

        gq_out[...] = reduced(SC, 0).astype(BF16)
        z_grad.start()

        z_hid[1][1].wait_send()
        z_hid[0][1].start()

        def own_part(r):
            acc_v[r, :] = mm(h_v[r, cols(0)], weight(SD, 0))

        each_tile(own_part)
        z_hid[1][0].wait_recv()
        z_hid[1][1].wait_recv()
        outer(SC, 1, ho_v, lambda: c_v[:, cols(1)])

        def output(r):
            total = mm(h_v[r, cols(1)], weight(SD, 1)) + mm(ho_v[r, cols(1)], weight(SC, 1))
            out_v[r, cols(1)] = total.astype(BF16)

        fold(SC, 1)
        each_tile(output)
        for k in (0, 1):
            x_back[k].wait_recv()

            def input_grad(r, k=k):
                total = mm_nt(pg_v[r, cols(k)], weight(FD, k)) + bf_in[r, cols(k)].astype(F32)
                ig_v[r, cols(k)] = total.astype(BF16)

            each_tile(input_grad)
        for f, g_v in ((SD, gsd_v), (FD, gfd_v), (FC, gfc_v)):
            for k in (0, 1):
                g_v[k] = reduced(f, k)

        z_grad.wait_recv()
        gsc_v[0] = gq_in[...].astype(F32)
        gsc_v[1] = reduced(SC, 1)
        for i, r in enumerate(halves):
            z_hid[0][i].wait_recv()
            out_v[r, cols(0)] = (acc_v[r, :] + mm(ho_v[r, cols(0)], weight(SC, 0))).astype(BF16)

        others(w_v.at[:, :, pl.ds(0, n_chips - 1), core], ag_send.at[0], ag_recv.at[0]).wait_send()
        others(scq_v.at[pl.ds(0, n_chips - 1), core], ag_send.at[1], ag_recv.at[4]).wait_send()
        pass_on_q().wait_send()
        others(w_v.at[:, :, :, core], tw_send.at[0], tw_recv.at[0]).wait_send()
        others(part_v.at[:, :, :, 1 - core], pr_send.at[0], pr_recv.at[0, 0]).wait_send()
        others(rs_v.at[:, :, pl.ds(0, n_chips - 1)], rs_send.at[0], rs_recv.at[0, 0]).wait_send()
        for copy in (z_shard, *z_hid[0], z_grad, x_in, *x_back):
            copy.wait_send()

    wide = (rows, 2 * width)
    dma = pltpu.SemaphoreType.DMA
    scratch = [
        pltpu.VMEM(wide, BF16),
        pltpu.VMEM(wide, BF16),
        pltpu.VMEM((4, 2, n_dp // 2, 2, shard, width), BF16),
        pltpu.VMEM((n_dp // 2, 2, shard, width), BF16),
        pltpu.VMEM(wide, BF16),
        pltpu.VMEM((rows, width), BF16),
        pltpu.VMEM((rows, width), BF16),
        pltpu.VMEM((rows, width), BF16),
        pltpu.VMEM(wide, F32),
        pltpu.VMEM(wide, BF16),
        pltpu.VMEM(wide, BF16),
        pltpu.VMEM(wide, BF16),
        pltpu.VMEM(wide, BF16),
        pltpu.VMEM(wide, BF16),
        pltpu.VMEM((4, 2, n_dp // 2, 2, shard, width), BF16),
        pltpu.VMEM((4, 2, n_dp // 2, shard, width), BF16),
        pltpu.VMEM((4, 2, n_dp // 2, shard, width), BF16),
        pltpu.VMEM((rows, width), F32),
        pltpu.VMEM((shard, width), BF16),
        pltpu.VMEM((shard, width), BF16),
        dma((6,)),
        dma((2,)),
        dma((5,)),
        dma((2,)),
        dma((5,)),
        dma((10,)),
        dma((10,)),
        dma((3,)),
        dma((3,)),
        dma((1,)),
        dma((4, 2)),
        dma((1,)),
        dma((4, 2)),
    ]
    return kernel, scratch


def hand_over(*refs):
    copies = [pltpu.make_async_copy(refs[i], refs[6 + i], refs[12].at[i]) for i in range(6)]
    for copy in copies:
        copy.start()
    for copy in copies:
        copy.wait()


def solution(mesh):
    n_dp, n_mp = mesh.shape["dp"], mesh.shape["mp"]

    def local(*args):
        rows, two_width = args[0].shape
        shard, width = args[2].shape[1:]
        kernel, scratch = make_kernel(n_dp, n_mp, rows, width, shard)
        act = jax.ShapeDtypeStruct((rows, two_width), BF16)
        grad = jax.ShapeDtypeStruct((2, shard, width), F32)
        hbm = pl.BlockSpec(memory_space=pl.ANY)
        shapes = (act, act, grad, grad, grad, grad)
        vmem = pl.BlockSpec(memory_space=pltpu.VMEM)
        args = [pltpu.with_memory_space_constraint(a, pltpu.HBM) for a in args]
        results = pl.pallas_call(
            kernel,
            out_shape=shapes,
            in_specs=[hbm] * 6,
            out_specs=[vmem] * 6,
            scratch_shapes=scratch,
            compiler_params=pltpu.CompilerParams(
                collective_id=0, has_side_effects=True, vmem_limit_bytes=48 * 1024 * 1024
            ),
            name="butterfly",
        )(*args)
        return pl.pallas_call(
            hand_over,
            out_shape=shapes,
            in_specs=[vmem] * 6,
            out_specs=[pl.BlockSpec(memory_space=pltpu.HBM)] * 6,
            scratch_shapes=[pltpu.SemaphoreType.DMA((6,))],
            compiler_params=pltpu.CompilerParams(vmem_limit_bytes=16 * 1024 * 1024),
            name="hand_over",
        )(*results)

    tokens = P("dp", "mp")
    blocks = P("mp", "dp", None)
    specs = (tokens, tokens, blocks, blocks, blocks, blocks)
    return jax.shard_map(local, mesh=mesh, in_specs=specs, out_specs=specs, check_vma=False)
```
